256 devices in a mesh: pipe: 8 (over z), dp: 2 (over y_lo), expert: 16 (over y_hi, x, core).
Axes of the slice: x: 4, y: 4 (y_hi: 2, y_lo: 2; y = y_hi * 2 + y_lo), z: 8, core: 2. Of those that a mesh axis runs over, the one named last changes fastest.
Arguments:
- layer_input: bfloat16 [8, 4096, 1536], P('pipe', ('dp', 'expert')), may hold values from -6 to 6
- handoff: bfloat16 [8, 4096, 1536], P('pipe', ('dp', 'expert')), may hold values from -6 to 6
- routes: int32 [8, 4096, 2], P('pipe', ('dp', 'expert')), may hold values from 0 to 7, all different within a row; in each aligned block of 128 rows (0 to 127, 128 to 255, ..., all dimensions but the last counted through in order) at most 48 rows name the same one
- gating: bfloat16 [8, 4096, 2], P('pipe', ('dp', 'expert')), may hold values from 0.19921875 to 1
- saved_pre: bfloat16 [8, 2, 16, 32, 48, 768], P('pipe', 'dp', 'expert'), may hold values from -6 to 6
- w_in: bfloat16 [8, 1536, 2, 16, 768], P('pipe', None, 'dp', 'expert'), may hold values from -0.15625 to 0.15625
- w_out: bfloat16 [8, 2, 16, 768, 1536], P('pipe', 'dp', 'expert'), may hold values from -0.109375 to 0.109375
Outputs:
- token_grad: bfloat16 [8, 4096, 1536], P('pipe', ('dp', 'expert'))
- w_in_grad: bfloat16 [8, 1536, 2, 16, 768], P('pipe', None, 'dp', 'expert')
- w_out_grad: bfloat16 [8, 2, 16, 768, 1536], P('pipe', 'dp', 'expert')
The draws below stay inside these ranges and needn't reach their ends.
Inputs may be any that keep to these rules, and one draw needn't show every extreme that they name: `routes`: each token names two different experts. In each block of 128 tokens (the tokens of one device) no expert is named more than 48 times, and in every block some expert is named exactly 48 times.
All inputs are finite; a program needn't handle non-finite values.
Results may differ from the reference program's by a relative error of at most 0.0049.
Values may be sent and summed in bfloat16 or wider, within the bound.
No kernel may reach another device: no remote copies, remote signals or barrier semaphores. Data moves between devices by JAX's collectives and lax.ppermute only.
A program may use at most 128 MiB of HBM per device.

```python
import math
import jax
import jax.numpy as jnp
import numpy as np
from jax import lax

D = 1536
F = 3072
TOK_DEV = 128
SECTIONS = 8
EXPERTS = 8
PANEL = 768
SOURCES = 32
TOKENS = 4096
CAP = 48
N_DP = 2
N_EXPERT = 16


def level_of(stream_key, dims, shards, low, top_value):
    loudness, own = 1.0, jax.random.fold_in(stream_key, 6)
    for dim, shards_of in shards:
        steps = jnp.exp(jax.random.uniform(jax.random.fold_in(own, dim), (shards_of,), jnp.float32, low / len(shards), top_value / len(shards)))
        loudness = loudness * jnp.repeat(steps, dims[dim] // shards_of).reshape([-1 if axis == dim else 1 for axis in range(len(dims))])
    return loudness


def shared_out(rng, own, number, rows, number_of, top, most, lean):
    sequence = jax.random.permutation(rng, number_of)
    packed, ordinary = shares(number_of, rows * top, most, lean, True), shares(number_of, rows * top, most, lean, False)
    places = jnp.arange(number_of)

    def named(lengths, rotation):
        used = int((lengths > 0).sum())
        fixed = max(1, used // 4)
        moved = fixed + (places - fixed + rotation * (used - fixed)) % max(1, number_of - fixed)
        return jnp.zeros((number_of,), jnp.int32).at[sequence[jnp.where(places < fixed, places, moved)]].set(jnp.asarray(lengths, jnp.int32))

    lengths = jnp.where(number % 4 == 0, named(packed, number // 4), named(ordinary, number - number // 4 - 1))
    mixed = jax.random.permutation(jax.random.fold_in(own, 3), number_of)
    source_of, sink = mixed[0:number_of // 2 * 2:2], mixed[1:number_of // 2 * 2:2]
    margin = jnp.minimum(lengths[source_of] - 1, most - lengths[sink]) // 2
    margin = jnp.where((source_of == sequence[0]) | (sink == sequence[0]) | (lengths[sink] == 0), 0, jnp.maximum(margin, 0))
    moved = jax.random.randint(jax.random.fold_in(own, 4), (number_of // 2,), 0, 1 << 20) % (margin + 1)
    lengths = lengths.at[source_of].add(-moved).at[sink].add(moved)
    members = jnp.searchsorted(jnp.cumsum(lengths), jnp.arange(rows * top), side="right").astype(jnp.int32)
    grid = members.reshape(top, rows).T
    grid = grid[jax.random.permutation(jax.random.fold_in(own, 1), rows)]
    rotation = jax.random.randint(jax.random.fold_in(own, 2), (rows, 1), 0, top)
    return jnp.take_along_axis(grid, (jnp.arange(top)[None, :] + rotation) % top, axis=1)


def shares(count, total, most, lean, full):
    weights = [(1 << 20) // math.isqrt(standing ** lean) + 1 for standing in range(1, count + 1)]
    largest = most if full else min(most, max(-(-total // count), total * weights[0] // sum(weights)))
    least = 1 if total - largest >= count - 1 else 0
    counts, rest = [largest] + [least] * (count - 1), total - largest - least * (count - 1)
    while rest > 0:
        free = [i for i in range(1, count) if counts[i] < largest] or [i for i in range(1, count) if counts[i] < most]
        whole, remaining = sum([weights[i] for i in free]), rest
        for i in free:
            extra = min(most - counts[i], max(1, remaining * weights[i] // whole), rest)
            counts[i] = counts[i] + extra
            rest = rest - extra
    return np.array(counts)


def noise(own_key, dims, scale, limit, split=(), held_as=jnp.bfloat16):
    drawn = scale * jax.random.normal(own_key, dims, jnp.float32)
    if split:
        drawn = drawn * level_of(own_key, dims, split, -0.22, 0.18)
    return jnp.clip(drawn, -limit, limit).astype(held_as)


def setup_inputs(seed: int = 0) -> dict:
    arg_keys = jax.random.split(jax.random.key(seed), 8)
    layer_input = noise(arg_keys[0], (SECTIONS, TOKENS, D), 1.0, 6.0, ((0, 8), (1, 32)))
    handoff = noise(arg_keys[1], (SECTIONS, TOKENS, D), 1.0, 6.0, ((0, 8), (1, 32)))
    routes_keys = jax.random.split(jax.random.fold_in(arg_keys[2], 1), SECTIONS * TOKENS // TOK_DEV)
    routes_turns = jax.random.permutation(jax.random.fold_in(arg_keys[2], 3), SECTIONS * TOKENS // TOK_DEV)
    routes = jax.vmap(lambda own, number: shared_out(jax.random.fold_in(arg_keys[2], 2), own, number, TOK_DEV, EXPERTS, 2, CAP, 2))(routes_keys, routes_turns).reshape((SECTIONS, TOKENS, 2))
    gating = jnp.clip(0.19921875 + 0.80078125 * jax.random.uniform(arg_keys[3], (SECTIONS, TOKENS, 2), jnp.float32) ** level_of(arg_keys[3], (SECTIONS, TOKENS, 2), ((0, 8), (1, 32)), -0.2, 0.2), 0.19921875, 1.0).astype(jnp.bfloat16)
    saved_pre = noise(arg_keys[4], (SECTIONS, N_DP, N_EXPERT, SOURCES, CAP, PANEL), 1.0, 6.0, ((0, 8), (1, 2), (2, 16)))
    w_in = noise(arg_keys[5], (SECTIONS, D, N_DP, N_EXPERT, PANEL), D ** -0.5, 0.15625, ((0, 8), (2, 2), (3, 16)))
    w_out = noise(arg_keys[6], (SECTIONS, N_DP, N_EXPERT, PANEL, D), F ** -0.5, 0.109375, ((0, 8), (1, 2), (2, 16)))
    return {"layer_input": layer_input, "handoff": handoff, "routes": routes, "gating": gating, "saved_pre": saved_pre, "w_in": w_in, "w_out": w_out}


root_two_pi = math.sqrt(2.0 / math.pi)
cubic_coef = 0.044715

def gelu_parts(values):
    inner_arg = root_two_pi * (values + cubic_coef * values * values * values)
    tangent = jnp.tanh(inner_arg)
    active = 0.5 * values * (1.0 + tangent)
    gelu_slope = 0.5 * (1.0 + tangent) + 0.5 * values * (1.0 - tangent * tangent) * root_two_pi * (1.0 + 3.0 * cubic_coef * values * values)
    return (active, gelu_slope)

def slot_table(route_block, expert_total, capacity):
    flat_ids = route_block.reshape(-1).astype(jnp.int32)
    pair_total = flat_ids.shape[0]
    onehot = (flat_ids[:, None] == jnp.arange(expert_total, dtype=jnp.int32)[None, :]).astype(jnp.int32)
    running = (jnp.cumsum(onehot, axis=0) - 1).astype(jnp.int32)
    position = lax.optimization_barrier(jnp.sum(running * onehot, axis=1)).astype(jnp.int32)
    slot_index = jnp.full((expert_total, capacity), pair_total, jnp.int32)
    slot_index = slot_index.at[flat_ids, position].set(jnp.arange(pair_total, dtype=jnp.int32))
    return (flat_ids, position, slot_index)

def fill_slots(source_rows, slot_index):
    padded = jnp.concatenate([source_rows, jnp.zeros((1, source_rows.shape[1]), source_rows.dtype)], axis=0)
    return padded[slot_index // 2]

def fill_gates(gate_block, slot_index):
    padded = jnp.concatenate([gate_block.reshape(-1), jnp.zeros((1,), gate_block.dtype)], axis=0)
    return padded[slot_index]

def one_expert(operands):
    input_rows, grad_rows, gate_rows, pre_rows, win_full, wout_full = operands
    upstream = jnp.dot(grad_rows, wout_full.T, preferred_element_type=jnp.float32)
    active, gelu_slope = gelu_parts(pre_rows.astype(jnp.float32))
    weight = gate_rows.astype(jnp.float32)[:, None]
    scaled = (weight * active).astype(jnp.bfloat16)
    pre_grad = (weight * upstream * gelu_slope).astype(jnp.bfloat16)
    out_grad = jnp.dot(scaled.T, grad_rows, preferred_element_type=jnp.float32)
    in_grad = jnp.dot(input_rows.T, pre_grad, preferred_element_type=jnp.float32)
    row_grad = jnp.dot(pre_grad, win_full.T, preferred_element_type=jnp.float32)
    return (in_grad, out_grad, row_grad)

def one_section(operands):
    inputs_sec, incoming_sec, routes_sec, gating_sec, saved_sec, win_sec, wout_sec = operands
    input_blocks = inputs_sec.reshape(SOURCES, TOK_DEV, D)
    grad_blocks = incoming_sec.reshape(SOURCES, TOK_DEV, D)
    route_blocks = routes_sec.reshape(SOURCES, TOK_DEV, 2)
    gate_blocks = gating_sec.reshape(SOURCES, TOK_DEV, 2)
    flat_ids, position, slot_index = jax.vmap(lambda route_block: slot_table(route_block, EXPERTS, CAP))(route_blocks)
    input_slots = jnp.transpose(jax.vmap(fill_slots)(input_blocks, slot_index), (1, 0, 2, 3)).reshape(EXPERTS, SOURCES * CAP, D)
    grad_slots = jnp.transpose(jax.vmap(fill_slots)(grad_blocks, slot_index), (1, 0, 2, 3)).reshape(EXPERTS, SOURCES * CAP, D)
    gate_slots = jnp.transpose(jax.vmap(fill_gates)(gate_blocks, slot_index), (1, 0, 2)).reshape(EXPERTS, SOURCES * CAP)
    pre_slots = jnp.transpose(saved_sec.reshape(N_DP, EXPERTS, 2, SOURCES, CAP, PANEL), (1, 3, 4, 0, 2, 5)).reshape(EXPERTS, SOURCES * CAP, F)
    win_full = jnp.transpose(win_sec.reshape(D, N_DP, EXPERTS, 2, PANEL), (2, 0, 1, 3, 4)).reshape(EXPERTS, D, F)
    wout_full = jnp.transpose(wout_sec.reshape(N_DP, EXPERTS, 2, PANEL, D), (1, 0, 2, 3, 4)).reshape(EXPERTS, F, D)
    in_grads, out_grads, row_grads = lax.map(one_expert, (input_slots, grad_slots, gate_slots, pre_slots, win_full, wout_full))
    win_grad = jnp.transpose(in_grads.reshape(EXPERTS, D, N_DP, 2, PANEL), (1, 2, 0, 3, 4)).reshape(D, N_DP, N_EXPERT, PANEL)
    wout_grad = jnp.transpose(out_grads.reshape(EXPERTS, N_DP, 2, PANEL, D), (1, 0, 2, 3, 4)).reshape(N_DP, N_EXPERT, PANEL, D)
    per_source = jnp.transpose(row_grads.reshape(EXPERTS, SOURCES, CAP, D), (1, 0, 2, 3)).reshape(SOURCES, EXPERTS * CAP, D)

    def collect(flat_rows, ids_block, position_block):
        picked = flat_rows[ids_block * CAP + position_block]
        return picked.reshape(TOK_DEV, 2, D).sum(axis=1)
    moe_grad = jax.vmap(collect)(per_source, flat_ids, position)
    token_out = (grad_blocks.astype(jnp.float32) + moe_grad).astype(jnp.bfloat16).reshape(TOKENS, D)
    return (token_out, win_grad.astype(jnp.bfloat16), wout_grad.astype(jnp.bfloat16))

def reference(layer_input, handoff, routes, gating, saved_pre, w_in, w_out):
    incoming = jnp.roll(handoff, -1, axis=0)
    token_grad, w_in_grad, w_out_grad = lax.map(one_section, (layer_input, incoming, routes, gating, saved_pre, w_in, w_out))
    return (token_grad, w_in_grad, w_out_grad)
```

```python
import math

import jax
import jax.numpy as jnp
from jax import lax
from jax.sharding import PartitionSpec as P

root_two_pi = math.sqrt(2.0 / math.pi)
cubic_coef = 0.044715


def gelu_parts(values):
    square = values * values
    tangent = jnp.tanh(root_two_pi * values * (1.0 + cubic_coef * square))
    half = 0.5 * (1.0 + tangent)
    slope = half + 0.5 * values * (1.0 - tangent * tangent) * root_two_pi * (
        1.0 + 3.0 * cubic_coef * square
    )
    return (values * half, slope)


def slot_keys(route_block, capacity):
    flat_ids = route_block.reshape(-1)
    pair_total = flat_ids.shape[0]
    order = jnp.arange(pair_total, dtype=jnp.int32)
    earlier = (flat_ids[:, None] == flat_ids[None, :]) & (order[:, None] < order[None, :])
    position = jnp.sum(earlier.astype(jnp.int32), axis=0)
    return (flat_ids * capacity + position).reshape(route_block.shape)


def on_device(layer_input, handoff, routes, gating, saved_pre, w_in, w_out):
    pipe_count = lax.axis_size("pipe")
    expert_count = lax.axis_size("expert")
    dp_count = lax.axis_size("dp")
    expert_total = expert_count // 2
    blocks, capacity, panel_size = saved_pre.shape[3:]
    model_width = w_in.shape[1]
    half = capacity // 2
    slots = expert_total * capacity
    everyone = ("dp", "expert")

    incoming = lax.ppermute(
        handoff, "pipe", [(s, (s - 1) % pipe_count) for s in range(pipe_count)]
    )
    grad_tokens = incoming[0]
    input_tokens = layer_input[0]
    keys = slot_keys(routes[0], capacity)
    slot_ids = jnp.arange(slots, dtype=jnp.int32)[:, None]
    first = slot_ids == keys[:, 0][None, :]
    second = slot_ids == keys[:, 1][None, :]
    chosen = (first | second).astype(jnp.bfloat16)
    gates = gating[0]
    zero = jnp.zeros((), jnp.bfloat16)
    gated = jnp.where(first, gates[:, 0][None, :], zero) + jnp.where(
        second, gates[:, 1][None, :], zero
    )

    def dispatch(select, tokens):
        rows = jnp.dot(select, tokens, preferred_element_type=jnp.float32).astype(jnp.bfloat16)
        rows = rows.reshape(1, expert_count, half, model_width)
        sent = jnp.broadcast_to(rows, (dp_count, expert_count, half, model_width))
        sent = sent.reshape(dp_count * expert_count, half, model_width)
        return lax.all_to_all(sent, everyone, split_axis=0, concat_axis=0, tiled=True)

    swap = [(e, e ^ 1) for e in range(expert_count)]

    def both(own):
        other = lax.ppermute(own, "expert", swap)
        return jnp.concatenate(
            [own.reshape(-1, own.shape[-1]), other.reshape(-1, own.shape[-1])], axis=0
        )

    grad_rows = both(dispatch(gated, grad_tokens))
    input_rows = both(dispatch(chosen, input_tokens))

    core = lax.axis_index("expert") % 2
    pre = saved_pre.reshape(blocks, 2, half, panel_size)
    pre_own = lax.dynamic_index_in_dim(pre, core, 1, keepdims=False)
    pre_other = lax.dynamic_index_in_dim(pre, 1 - core, 1, keepdims=False)
    pre_rows = jnp.concatenate([pre_own, pre_other], axis=0).reshape(-1, panel_size)
    win = w_in.reshape(model_width, panel_size)
    wout = w_out.reshape(panel_size, model_width)

    upstream = jnp.einsum("rd,hd->rh", grad_rows, wout, preferred_element_type=jnp.float32)
    active, slope = gelu_parts(pre_rows.astype(jnp.float32))
    pre_grad = (upstream * slope).astype(jnp.bfloat16)
    row_grad = jnp.einsum("rh,dh->rd", pre_grad, win, preferred_element_type=jnp.float32)
    row_total = blocks * half
    mine = row_grad[:row_total]
    theirs = row_grad[row_total:].astype(jnp.bfloat16)
    summed = mine + lax.ppermute(theirs, "expert", swap).astype(jnp.float32)
    back = lax.all_to_all(
        summed.astype(jnp.bfloat16).reshape(blocks, half, model_width),
        everyone,
        split_axis=0,
        concat_axis=0,
        tiled=True,
    )
    out_grad = jnp.einsum(
        "rh,rd->hd", active.astype(jnp.bfloat16), grad_rows, preferred_element_type=jnp.float32
    )
    in_grad = jnp.einsum("rd,rh->dh", input_rows, pre_grad, preferred_element_type=jnp.float32)

    back = back.reshape(dp_count, slots, model_width)
    moe_grad = jnp.einsum(
        "st,psd->td", chosen, back, preferred_element_type=jnp.float32
    )
    token_grad = (grad_tokens.astype(jnp.float32) + moe_grad).astype(jnp.bfloat16)[None]
    return (
        token_grad,
        in_grad.astype(jnp.bfloat16).reshape(w_in.shape),
        out_grad.astype(jnp.bfloat16).reshape(w_out.shape),
    )


def solution(mesh):
    in_specs = (
        P("pipe", ("dp", "expert"), None),
        P("pipe", ("dp", "expert"), None),
        P("pipe", ("dp", "expert"), None),
        P("pipe", ("dp", "expert"), None),
        P("pipe", "dp", "expert", None, None, None),
        P("pipe", None, "dp", "expert", None),
        P("pipe", "dp", "expert", None, None),
    )
    out_specs = (
        P("pipe", ("dp", "expert"), None),
        P("pipe", None, "dp", "expert", None),
        P("pipe", "dp", "expert", None, None),
    )
    return jax.shard_map(
        on_device, mesh=mesh, in_specs=in_specs, out_specs=out_specs, check_vma=False
    )
```

```python
import math

import jax
import jax.numpy as jnp
import numpy as np
from jax import lax
from jax.experimental import pallas as pl
from jax.experimental.pallas import tpu as pltpu
from jax.sharding import PartitionSpec as P

root_two_pi = math.sqrt(2.0 / math.pi)
cubic_coef = 0.044715
SIDE = 4
ARRIVAL = (1, 3, 2)
TURN = (0, 2, 3, 1)
TILE = 256
WIDE = 256
SPAN = 256


def gelu_parts(values):
    square = values * values
    tangent = jnp.tanh(root_two_pi * values * (1.0 + cubic_coef * square))
    half = 0.5 * (1.0 + tangent)
    slope = half + 0.5 * values * (1.0 - tangent * tangent) * root_two_pi * (
        1.0 + 3.0 * cubic_coef * square
    )
    return (values * half, slope)


def place(x, y, core):
    return (y % 2) * (SIDE * SIDE) + (y // 2) * (2 * SIDE) + x * 2 + core


def send(value, x_core, x_steps, y_steps):
    pairs = []
    for x in range(SIDE):
        for y in range(SIDE):
            for core in range(2):
                to_x = (x + x_steps) % SIDE if core == x_core else x
                to_y = y if core == x_core else (y + y_steps) % SIDE
                pairs.append((place(x, y, core), place(to_x, to_y, core)))
    return lax.ppermute(value, ("dp", "expert"), pairs)


def send_second(value, k):
    return send(value, 1, TURN[k], k)


def send_back(value, k):
    return send(value, 1, -TURN[k], -k)


def swap_cores(value):
    count = lax.axis_size("expert")
    return lax.ppermute(value, "expert", [(e, e ^ 1) for e in range(count)])


def first_stage(value):
    return [value] + [send(value, 0, k, k) for k in range(1, SIDE)]


def weight_grad(left, right):
    height, width = left[0].shape[1], right[0].shape[1]

    def body(*refs):
        lefts, rights, out_ref = refs[: len(left)], refs[len(left) : -1], refs[-1]
        across = width // WIDE

        def tile(i, carry):
            here = pl.ds(pl.multiple_of(i // across * TILE, TILE), TILE)
            there = pl.ds(pl.multiple_of(i % across * WIDE, WIDE), WIDE)
            tall = jnp.concatenate([ref[:, here] for ref in lefts], axis=0)
            flat = jnp.concatenate([ref[:, there] for ref in rights], axis=0)
            out_ref[here, there] = lax.dot_general(
                tall, flat, (((0,), (0,)), ((), ())), preferred_element_type=jnp.float32
            ).astype(jnp.bfloat16)
            return carry

        lax.fori_loop(0, height // TILE * across, tile, 0)

    held = pl.BlockSpec(memory_space=pltpu.VMEM)
    return pl.pallas_call(
        body,
        out_shape=jax.ShapeDtypeStruct((height, width), jnp.bfloat16),
        in_specs=[held] * (len(left) + len(right)),
        out_specs=held,
        compiler_params=pltpu.CompilerParams(vmem_limit_bytes=24 << 20),
    )(*left, *right)


def make_tags(choices, gates, capacity, expert_total):
    token_total = choices.shape[1]

    def body(choice_ref, gate_ref, out_ref):
        experts = lax.broadcasted_iota(jnp.int32, (expert_total, token_total), 0)
        picked = [experts == choice_ref[k : k + 1, :] for k in range(2)]
        named = jnp.where(picked[0] | picked[1], 1.0, 0.0).astype(jnp.bfloat16)
        row = lax.broadcasted_iota(jnp.int32, (token_total, token_total), 0)
        column = lax.broadcasted_iota(jnp.int32, (token_total, token_total), 1)
        earlier = jnp.where(row < column, 1.0, 0.0).astype(jnp.bfloat16)
        counts = jnp.dot(named, earlier, preferred_element_type=jnp.float32)
        starts = (experts * capacity).astype(jnp.float32)
        for k in range(2):
            out_ref[k : k + 1, :] = jnp.sum(
                jnp.where(picked[k], starts + counts, 0.0), axis=0, keepdims=True
            )
        out_ref[2:4, :] = gate_ref[...].astype(jnp.float32)

    held = pl.BlockSpec(memory_space=pltpu.VMEM)
    return pl.pallas_call(
        body,
        out_shape=jax.ShapeDtypeStruct((4, token_total), jnp.float32),
        in_specs=[held, held],
        out_specs=held,
        compiler_params=pltpu.CompilerParams(vmem_limit_bytes=4 << 20),
        name="tags",
    )(choices, gates)


def order_table():
    table = np.zeros((2 * SIDE * SIDE, SIDE + 2 * SIDE * SIDE), np.int32)
    for x in range(SIDE):
        for y in range(SIDE):
            for core in range(2):
                row = table[place(x, y, core)]
                for k in range(SIDE):
                    to_x = x if core == 0 else (x + TURN[k]) % SIDE
                    to_y = (y + k) % SIDE if core == 0 else y
                    row[k] = (to_y // 2) * SIDE + to_x
                    for j in range(SIDE):
                        at = SIDE + k * SIDE + j
                        by_y = place((x - j) % SIDE, (y - k) % SIDE, 0)
                        by_x = place((x - TURN[k]) % SIDE, (y - j) % SIDE, 1)
                        row[at] = by_x if core else by_y
                        row[at + SIDE * SIDE] = by_y if core else by_x
    return table


def selector(experts_ref, tag_ref, capacity, gated):
    token_total = tag_ref.shape[1]
    slot = lax.broadcasted_iota(jnp.int32, (capacity, token_total), 0)
    keys = tag_ref[0:2, :].astype(jnp.int32)
    gates = tag_ref[2:4, :] if gated else jnp.ones((2, token_total), jnp.float32)
    pieces = []
    for k in range(SIDE):
        local = keys - experts_ref[k] * capacity
        pieces.append(
            jnp.where(slot == local[0:1, :], gates[0:1, :], 0.0)
            + jnp.where(slot == local[1:2, :], gates[1:2, :], 0.0)
        )
    return jnp.concatenate(pieces, axis=0).astype(jnp.bfloat16)


def held_call(body, out_shape, experts, operands):
    held = pl.BlockSpec(memory_space=pltpu.VMEM)
    return pl.pallas_call(
        body,
        out_shape=out_shape,
        in_specs=[pl.BlockSpec(memory_space=pltpu.SMEM)] + [held] * len(operands),
        out_specs=tuple(held for _ in out_shape),
        compiler_params=pltpu.CompilerParams(vmem_limit_bytes=20 << 20),
    )(experts, *operands)


def pick_slots(experts, tags, tokens, capacity, gated):
    width = tokens[0].shape[1]

    def body(experts_ref, *refs):
        tag_refs, token_refs, out_refs = refs[:SIDE], refs[SIDE : 2 * SIDE], refs[2 * SIDE :]
        selects = [selector(experts_ref, ref, capacity, gated) for ref in tag_refs]

        def columns(i, carry):
            here = pl.ds(pl.multiple_of(i * SPAN, SPAN), SPAN)
            for j in range(SIDE):
                rows = jnp.dot(
                    selects[j], token_refs[j][:, here], preferred_element_type=jnp.float32
                ).astype(jnp.bfloat16)
                for k in range(SIDE):
                    out_refs[k][pl.ds(j * capacity, capacity), here] = rows[
                        k * capacity : (k + 1) * capacity
                    ]
            return carry

        lax.fori_loop(0, width // SPAN, columns, 0)

    shape = jax.ShapeDtypeStruct((SIDE * capacity, width), jnp.bfloat16)
    return held_call(body, (shape,) * SIDE, experts, tuple(tags) + tuple(tokens))


def combine_slots(experts, tags, returned, grad_tokens, capacity):
    token_total, width = grad_tokens.shape

    def body(experts_ref, *refs):
        tag_refs, row_refs = refs[:SIDE], refs[SIDE : 2 * SIDE]
        grad_ref, out_refs = refs[2 * SIDE], refs[2 * SIDE + 1 :]
        selects = [selector(experts_ref, ref, capacity, False) for ref in tag_refs]

        def columns(i, carry):
            here = pl.ds(pl.multiple_of(i * SPAN, SPAN), SPAN)
            for j in range(SIDE):
                rows = jnp.concatenate(
                    [ref[pl.ds(j * capacity, capacity), here] for ref in row_refs], axis=0
                )
                sums = lax.dot_general(
                    selects[j], rows, (((0,), (0,)), ((), ())), preferred_element_type=jnp.float32
                )
                if j == 0:
                    out_refs[0][:, here] = sums + grad_ref[:, here].astype(jnp.float32)
                else:
                    out_refs[j][:, here] = sums.astype(jnp.bfloat16)
            return carry

        lax.fori_loop(0, width // SPAN, columns, 0)

    shapes = [jax.ShapeDtypeStruct((token_total, width), jnp.float32)]
    shapes += [jax.ShapeDtypeStruct((token_total, width), jnp.bfloat16)] * (SIDE - 1)
    return held_call(body, tuple(shapes), experts, tuple(tags) + tuple(returned) + (grad_tokens,))


def section(layer_input, handoff, routes, gating, saved_pre, w_in, w_out):
    pipe_count = lax.axis_size("pipe")
    blocks, capacity, panel_size = saved_pre.shape[3:]
    model_width = w_in.shape[1]
    wide = jnp.float32
    narrow = jnp.bfloat16
    chunk = SIDE * capacity

    dp_index = lax.axis_index("dp")
    expert_index = lax.axis_index("expert")
    device = dp_index * lax.axis_size("expert") + expert_index
    spot = lax.dynamic_index_in_dim(jnp.asarray(order_table()), device, 0, keepdims=False)

    incoming = lax.ppermute(handoff, "pipe", [(s, (s - 1) % pipe_count) for s in range(pipe_count)])
    grad_tokens = incoming[0]
    input_blocks = first_stage(layer_input[0])
    tags = make_tags(routes[0].T, gating[0].T, capacity, lax.axis_size("expert") // 2)
    tag_blocks = first_stage(tags)
    grad_blocks = first_stage(grad_tokens)

    experts, orders = spot[:SIDE], spot[SIDE:]
    grad_own = list(pick_slots(experts, tag_blocks, grad_blocks, capacity, True))
    input_own = list(pick_slots(experts, tag_blocks, input_blocks, capacity, False))
    for k in ARRIVAL:
        grad_own[k] = send_second(grad_own[k], k)
        input_own[k] = send_second(input_own[k], k)
    input_sib = []
    for k in range(SIDE):
        pieces = 1
        rows = chunk // pieces
        for piece in range(pieces):
            input_sib.append(swap_cores(input_own[k][piece * rows : (piece + 1) * rows]))

    pre_blocks = saved_pre.reshape(blocks, capacity, panel_size)
    ordered = pre_blocks.at[orders].get(mode="promise_in_bounds")
    ordered = lax.optimization_barrier(ordered.reshape(2 * SIDE * chunk, panel_size))
    actives = [gelu_parts(ordered.astype(wide))[0].astype(narrow)]
    win = w_in.reshape(model_width, panel_size)
    wout = w_out.reshape(panel_size, model_width)

    def hidden(grad_rows, side, at):
        upstream = jnp.einsum("rd,hd->rh", grad_rows, wout, preferred_element_type=wide)
        values = ordered[(side * SIDE + at) * chunk : (side * SIDE + at + 1) * chunk]
        return (upstream * gelu_parts(values.astype(wide))[1]).astype(narrow)

    def to_model(pre_grad):
        return jnp.einsum("rh,dh->rd", pre_grad, win, preferred_element_type=wide)

    back = [None] * SIDE
    grad_sib = [None] * SIDE
    hidden_own = [None] * SIDE
    hidden_sib = [None] * SIDE
    for k in (0,) + ARRIVAL:
        grad_sib[k] = swap_cores(grad_own[k])
        hidden_own[k] = hidden(grad_own[k], 0, k)
        hidden_sib[k] = hidden(grad_sib[k], 1, k)
        rows_sib = to_model(hidden_sib[k]).astype(narrow)
        theirs = swap_cores(rows_sib)
        part = (to_model(hidden_own[k]) + theirs.astype(wide)).astype(narrow)
        part = send_back(part, k) if k else part
        back[k] = part

    out_grad = weight_grad(actives, grad_own + grad_sib)
    in_grad = weight_grad(input_own + input_sib, hidden_own + hidden_sib)

    partial = combine_slots(experts, tag_blocks, back, grad_tokens, capacity)
    total = partial[0]
    for j in ARRIVAL:
        total = total + send(partial[j], 0, -j, -j).astype(wide)
    return (
        total.astype(narrow)[None],
        in_grad.reshape(w_in.shape),
        out_grad.reshape(w_out.shape),
    )


def solution(mesh):
    in_specs = (
        P("pipe", ("dp", "expert"), None),
        P("pipe", ("dp", "expert"), None),
        P("pipe", ("dp", "expert"), None),
        P("pipe", ("dp", "expert"), None),
        P("pipe", "dp", "expert", None, None, None),
        P("pipe", None, "dp", "expert", None),
        P("pipe", "dp", "expert", None, None),
    )
    out_specs = (
        P("pipe", ("dp", "expert"), None),
        P("pipe", None, "dp", "expert", None),
        P("pipe", "dp", "expert", None, None),
    )
    return jax.shard_map(
        section, mesh=mesh, in_specs=in_specs, out_specs=out_specs, check_vma=False
    )
```
